32 devices in a mesh: groups: 2 (over y), out: 4 (over z), inp: 4 (over x, core).
Axes of the slice: x: 2, y: 2, z: 4, core: 2. Of those that a mesh axis runs over, the one named last changes fastest.
Arguments:
- acts_rot: bfloat16 [64, 8192], P(('groups', 'out', 'inp')), parts along dimension 0, may hold values from -6 to 6
- grads_rot: bfloat16 [64, 28672], P(('groups', 'out', 'inp')), parts along dimension 0, may hold values from -0.00024414062 to 0.00024414062
- query_grads: bfloat16 [8, 128, 28672], P('groups', None, 'out'), parts along dimension 0, may hold values from -6 to 6
- query_acts: bfloat16 [8, 128, 8192], P('groups', 'out', 'inp'), parts along dimension 0, may hold values from -0.5 to 0.5
- eigen: bfloat16 [28672, 8192], P('out', 'inp'), may hold values from 0.049804688 to 5
- block_mask: int32 [8, 224, 64], P('groups'), parts along dimension 0, may hold values from 0 to 1, as said below
- order: int32 [64], P('groups'), parts along dimension 0, may hold values from 0 to 31, each once
- segment_ids: int32 [64], P('groups'), parts along dimension 0, may hold values from 0 to 3, never falling along the last dimension, each value on 1 to 16 neighbouring positions
Outputs:
- token_scores: float32 [4, 64], P(None, 'groups'), parts along dimension 1
- seq_scores: float32 [8, 4], P('groups'), parts along dimension 0
The draws below stay inside these ranges and needn't reach their ends.
There are 2 independent parts, one for each index of `groups`. The reference program is written for one: setup_inputs(seed, part) draws one part's arguments, and reference() takes and returns one part's arrays. A program takes and returns all parts, laid end to end along the dimension named above; an argument that names none is the same for every part. Nothing has to cross between parts.
Inputs may be any that keep to these rules, and one draw needn't show every extreme that they name: block_mask[q, r, c] is 1 where query q keeps the block of rows r * 128 to r * 128 + 127 and columns c * 128 to c * 128 + 127, else 0. order holds each of the 32 positions once. segment_ids never falls along the positions; each sequence has 1 to 16 positions and one has exactly 16.
All inputs are finite; a program needn't handle non-finite values.
Results may differ from the reference program's by a relative error of at most 0.0035.
Values may be sent and summed in bfloat16 or wider, within the bound.
No kernel may reach another device: no remote copies, remote signals or barrier semaphores. Data moves between devices by JAX's collectives and lax.ppermute only.
A program may use at most 512 MiB of HBM per device.

```python
import math
import jax
import jax.numpy as jnp
import numpy as np
from jax import lax

OUT = 28672
IN = 8192
BLOCK = 128
Q = 4
QT = 128
SEQS = 4
TOKENS = 32


def draw_block_mask(key, part):
    level_key = jax.random.fold_in(key, 11)
    cell_key = jax.random.fold_in(key, 23)
    levels = jax.random.randint(level_key, (Q, OUT // BLOCK, 1), 50, 451)
    cells = jax.random.randint(cell_key, (Q, OUT // BLOCK, IN // BLOCK), 0, 1000)
    return (cells < levels).astype(jnp.int32)


def block_levels(rng, shape, split, least, top_value):
    gain = 1.0
    for position, parts in split:
        draws = jax.random.uniform(jax.random.fold_in(jax.random.fold_in(rng, 6), position), (parts,), jnp.float32, least / len(split), top_value / len(split))
        gain = gain * jnp.repeat(jnp.exp(draws), shape[position] // parts).reshape((-1,) + (1,) * (len(shape) - 1 - position))
    return gain


def profile(number_of, total, most, lean):
    portions = [(1 << 20) // math.isqrt(grade ** lean) + 1 for grade in range(2, number_of + 1)]
    spare, holding = total - most - (number_of - 1), [1] * (number_of - 1)
    while spare > 0:
        free = [i for i in range(number_of - 1) if holding[i] < most]
        mass, remaining = sum([portions[i] for i in free]), spare
        for i in free:
            addition = min(most - holding[i], max(1, remaining * portions[i] // mass), spare)
            holding[i] = holding[i] + addition
            spare = spare - addition
    return np.array([most] + holding)


def ragged(stream_key, amount, total, bound, slope):
    if amount == 2:
        one = jax.random.randint(stream_key, (), max(1, total - bound), min(bound, total - 1) + 1)
        return jnp.stack([one, total - one])
    sizes = jnp.asarray(profile(amount, total, bound, slope), jnp.int32)
    twos = (amount - 1) // 2
    source_of, taker = sizes[1:1 + 2 * twos:2], sizes[2:2 + 2 * twos:2]
    room = jnp.minimum(source_of - 1, bound - taker)
    passed = jax.random.randint(jax.random.fold_in(stream_key, 1), (twos,), 0, 1 << 20) % (room + 1)
    sizes = sizes.at[1:1 + 2 * twos:2].set(source_of - passed).at[2:2 + 2 * twos:2].set(taker + passed)
    return sizes[jax.random.permutation(jax.random.fold_in(stream_key, 2), amount)]


def gaussian(stream_key, dims, scale, bound, cuts=(), kind=jnp.bfloat16):
    array = jax.random.normal(stream_key, dims, jnp.float32) * scale
    if len(cuts) > 0:
        array = block_levels(stream_key, dims, cuts, -0.22, 0.18) * array
    return jnp.clip(array, min=-bound, max=bound).astype(kind)


def setup_inputs(seed: int = 0, part: int = 0) -> dict:
    seeds = jax.random.split(jax.random.key(seed), 9)
    part_splits = jax.random.split(jax.random.fold_in(seeds[8], part), 9)
    return {
        "acts_rot": gaussian(part_splits[0], (TOKENS, IN), 1.0, 6.0, ((0, 16),)),
        "grads_rot": gaussian(part_splits[1], (TOKENS, OUT), (2 * OUT * IN) ** -0.5, 0.00024414062, ((0, 16),)),
        "query_grads": gaussian(part_splits[2], (Q, QT, OUT), 1.0, 6.0, ((2, 4),)),
        "query_acts": gaussian(part_splits[3], (Q, QT, IN), QT ** -0.5, 0.5, ((1, 4), (2, 4))),
        "eigen": jnp.clip(jnp.exp(math.log(5.0) - 4.609084 * jax.random.uniform(seeds[4], (OUT, IN), jnp.float32) ** block_levels(seeds[4], (OUT, IN), ((0, 4), (1, 4)), -0.2, 0.2)), 0.049804688, 5.0).astype(jnp.bfloat16),
        "block_mask": draw_block_mask(jax.random.fold_in(jax.random.fold_in(seeds[8], part), 71), part),
        "order": jax.random.permutation(part_splits[6], TOKENS).astype(jnp.int32),
        "segment_ids": jnp.searchsorted(jnp.cumsum(ragged(part_splits[7], SEQS, TOKENS, TOKENS // 2, 1)), jnp.arange(TOKENS), side="right").astype(jnp.int32),
    }


damping = 0.1


def reference(acts_rot, grads_rot, query_grads, query_acts, eigen, block_mask, order, segment_ids):
    strip_rows = 8 * BLOCK
    acts_float = acts_rot.astype(jnp.float32)
    query_float = query_acts.astype(jnp.float32)

    def one_strip(strip_index):
        first_row = (strip_index * strip_rows).astype(jnp.int32)
        grad_query = lax.dynamic_slice_in_dim(query_grads, first_row, strip_rows, 2).astype(jnp.float32)
        outer_sum = jnp.einsum("qsi,qsj->qij", grad_query, query_float)
        eigen_strip = lax.dynamic_slice_in_dim(eigen, first_row, strip_rows, 0).astype(jnp.float32)
        mask_strip = lax.dynamic_slice_in_dim(block_mask, (strip_index * 8).astype(jnp.int32), 8, 1)
        kept_mask = jnp.repeat(jnp.repeat(mask_strip, BLOCK, axis=1), BLOCK, axis=2) > 0
        precond = jnp.where(kept_mask, outer_sum / (eigen_strip + damping), 0.0).astype(jnp.bfloat16)
        image_part = jnp.einsum("tj,qij->qti", acts_float, precond.astype(jnp.float32))
        grad_strip = lax.dynamic_slice_in_dim(grads_rot, first_row, strip_rows, 1).astype(jnp.float32)
        return jnp.sum(image_part * grad_strip[None], axis=2)

    strip_scores = lax.map(one_strip, jnp.arange(OUT // strip_rows, dtype=jnp.int32))
    score_total = jnp.sum(strip_scores, axis=0)
    token_scores = jnp.zeros_like(score_total).at[:, order].set(score_total)
    member = (segment_ids[:, None] == jnp.arange(SEQS, dtype=jnp.int32)[None, :]).astype(jnp.float32)
    seq_scores = jnp.dot(token_scores, member, precision=lax.Precision.HIGHEST)
    return token_scores, seq_scores
```

```python
import functools
import math

import jax
import jax.numpy as jnp
from jax import lax
from jax.experimental import pallas as pl
from jax.experimental.pallas import tpu as pltpu
from jax.sharding import PartitionSpec as P


BLOCK = 128
SEQS = 4
UNROLL = 8
CHUNKS = 2

damping = 0.1


def turn_kernel(in_ref, out_ref):
    for q in range(in_ref.shape[0]):
        out_ref[q] = in_ref[q].T


def turn(query_grads, tile):
    queries, tokens, rows = query_grads.shape
    return pl.pallas_call(
        turn_kernel,
        grid=(rows // tile,),
        in_specs=[pl.BlockSpec((queries, tokens, tile), lambda i: (0, 0, i))],
        out_specs=pl.BlockSpec((queries, tile, tokens), lambda i: (0, i, 0)),
        out_shape=jax.ShapeDtypeStruct((queries, rows, tokens), query_grads.dtype),
        compiler_params=pltpu.CompilerParams(dimension_semantics=("arbitrary",)),
    )(query_grads)


def score_kernel(
    unit, first_col, shard_count,
    place_ref, count_ref, grad_row_ref, row_ref, col_a_ref, col_b_ref, slot_a_ref, slot_b_ref,
    eigen_ref, turned_ref, grads_ref, acts_ref, map_ref, base_ref, *rest,
):
    shards = rest[:shard_count]
    out_ref, weights_ref, grads_scr, sums_ref = rest[shard_count:]
    step = pl.program_id(0)
    queries, tile, _ = turned_ref.shape
    width = eigen_ref.shape[1]
    col_blocks = width // BLOCK
    length = row_ref.shape[0] // pl.num_programs(0)
    row_units = tile // unit

    @pl.when(step == 0)
    def _():
        sums_ref[...] = jnp.zeros_like(sums_ref)
        weights_ref[queries * col_blocks] = jnp.zeros(weights_ref.shape[1:], weights_ref.dtype)
        for k, shard in enumerate(shards):
            held = shard.shape[1]
            place = pl.multiple_of(place_ref[k] * held, held)
            for q in range(queries):
                for c in range(col_blocks):
                    weights_ref[q * col_blocks + c, pl.ds(place, held), :] = shard[
                        q, :, c * BLOCK : (c + 1) * BLOCK
                    ]

    for r in range(row_units):
        grads_scr[r] = grads_ref[:, r * unit : (r + 1) * unit]

    def pass_over(k, carry):
        start = step * length + k * UNROLL
        for u in range(UNROLL):
            at = start + u
            slot_a, slot_b = slot_a_ref[at], slot_b_ref[at]
            row = row_ref[at]
            grad_row = pl.multiple_of(grad_row_ref[at], unit)
            rows = pl.ds(pl.multiple_of(row * unit, unit), unit)
            cols_a = pl.ds(pl.multiple_of(col_a_ref[at], BLOCK), BLOCK)
            cols_b = pl.ds(pl.multiple_of(col_b_ref[at], BLOCK), BLOCK)
            left = turned_ref.reshape(queries * tile, turned_ref.shape[2])[pl.ds(grad_row, unit), :]
            right = jnp.concatenate([weights_ref[slot_a], weights_ref[slot_b]], axis=1)
            outer = jnp.dot(left, right, preferred_element_type=jnp.float32)
            scale_a = 1.0 / (eigen_ref[rows, cols_a].astype(jnp.float32) + damping)
            scale_b = 1.0 / (eigen_ref[rows, cols_b].astype(jnp.float32) + damping)
            precond = jnp.concatenate(
                [
                    (outer[:, :BLOCK] * scale_a).astype(jnp.bfloat16),
                    (outer[:, BLOCK:] * scale_b).astype(jnp.bfloat16),
                ],
                axis=1,
            )
            part = jnp.dot(grads_scr[row], precond, preferred_element_type=jnp.float32)
            sums_ref[slot_a] += part[:, :BLOCK]
            sums_ref[slot_b] += part[:, BLOCK:]
        return carry

    lax.fori_loop(0, count_ref[step], pass_over, 0)

    @pl.when(step == pl.num_programs(0) - 1)
    def _():
        for q in range(queries):
            total = sums_ref[q * col_blocks] * acts_ref[:, :BLOCK].astype(jnp.float32)
            for c in range(1, col_blocks):
                total += sums_ref[q * col_blocks + c] * acts_ref[
                    :, c * BLOCK : (c + 1) * BLOCK
                ].astype(jnp.float32)
            score = jnp.sum(total, axis=1, keepdims=True)
            mapped = jnp.sum(score * map_ref[...], axis=0, keepdims=True)
            out_ref[q : q + 1, :] = base_ref[q : q + 1, :] + mapped


def block_lists(mask, unit, tile_units, col_blocks):
    queries, row_units, _ = mask.shape
    tiles = row_units // tile_units
    half = (col_blocks + 1) // 2
    kept = mask.astype(jnp.int32)
    col = jnp.arange(col_blocks, dtype=jnp.int32)
    rank = jnp.sum(jnp.where(col[None, :] < col[:, None], kept[:, :, None, :], 0), axis=3)
    pair = jnp.arange(half, dtype=jnp.int32)[:, None]
    first = mask[:, :, None, :] & (rank[:, :, None, :] == 2 * pair)
    second = mask[:, :, None, :] & (rank[:, :, None, :] == 2 * pair + 1)
    col_a = jnp.sum(jnp.where(first, col, 0), axis=3)
    col_b = jnp.sum(jnp.where(second, col, 0), axis=3)
    has_a = jnp.sum(kept, axis=2)[:, :, None] > 2 * pair[:, 0]
    has_b = jnp.sum(kept, axis=2)[:, :, None] > 2 * pair[:, 0] + 1
    col_b = jnp.where(has_b, col_b, col_a)
    query = jnp.arange(queries, dtype=jnp.int32)[:, None, None]
    row = (jnp.arange(row_units, dtype=jnp.int32) % tile_units)[None, :, None]
    code = (((query * tile_units + row) * col_blocks + col_a) * col_blocks + col_b) * 2 + has_b.astype(jnp.int32)

    def by_tile(x):
        x = x.reshape(queries, tiles, tile_units, half)
        return x.transpose(1, 0, 2, 3).reshape(tiles, queries * tile_units * half)

    code, valid = by_tile(code), by_tile(has_a)
    entries = code.shape[1]
    length = -(-entries // UNROLL) * UNROLL
    at = jnp.arange(entries, dtype=jnp.int32)
    place = jnp.sum(jnp.where(at[None, :] < at[:, None], valid[:, None, :].astype(jnp.int32), 0), axis=2)
    slots = jnp.arange(length, dtype=jnp.int32)
    hit = valid[:, None, :] & (place[:, None, :] == slots[None, :, None])
    packed = jnp.sum(jnp.where(hit, code[:, None, :] + 1, 0), axis=2)
    there = packed > 0
    packed = jnp.maximum(packed - 1, 0)
    total = jnp.sum(valid.astype(jnp.int32), axis=1)
    spare = queries * col_blocks
    has_b = there & (packed % 2 == 1)
    rest = packed // 2
    col_b = rest % col_blocks
    rest = rest // col_blocks
    col_a = rest % col_blocks
    rest = rest // col_blocks
    row = rest % tile_units
    query = rest // tile_units
    slot_a = jnp.where(there, query * col_blocks + col_a, spare)
    slot_b = jnp.where(has_b, query * col_blocks + col_b, spare)
    grad_row = (query * tile_units + row) * unit
    return [-(-total // UNROLL)] + [
        x.reshape(-1) for x in (grad_row, row, col_a * BLOCK, col_b * BLOCK, slot_a, slot_b)
    ]


def score_part(lists, eigen, turned, shards, places, grads, acts, mapping, base, unit, tile, first_col, width):
    queries, rows, query_tokens = turned.shape
    tokens = grads.shape[0]
    col_blocks = width // BLOCK
    first = first_col // width
    kernel = functools.partial(score_kernel, unit, first_col, len(shards))
    whole = lambda shape: pl.BlockSpec(shape, lambda i, *_: (0,) * len(shape))
    return pl.pallas_call(
        kernel,
        grid_spec=pltpu.PrefetchScalarGridSpec(
            num_scalar_prefetch=8,
            grid=(rows // tile,),
            in_specs=[
                pl.BlockSpec((tile, width), lambda i, *_: (i, first)),
                pl.BlockSpec((queries, tile, query_tokens), lambda i, *_: (0, i, 0)),
                pl.BlockSpec((tokens, tile), lambda i, *_: (0, i)),
                pl.BlockSpec((tokens, width), lambda i, *_: (0, first)),
                whole(mapping.shape),
                whole(base.shape),
                *[whole(s.shape) for s in shards],
            ],
            out_specs=whole(base.shape),
            scratch_shapes=[
                pltpu.VMEM((queries * col_blocks + 1, query_tokens, BLOCK), jnp.bfloat16),
                pltpu.VMEM((tile // unit, tokens, unit), jnp.bfloat16),
                pltpu.VMEM((queries * col_blocks + 1, tokens, BLOCK), jnp.float32),
            ],
        ),
        out_shape=jax.ShapeDtypeStruct(base.shape, jnp.float32),
        compiler_params=pltpu.CompilerParams(
            dimension_semantics=("arbitrary",), vmem_limit_bytes=48 << 20
        ),
    )(places, *lists, eigen, turned, grads, acts, mapping, base, *shards)


def is_small_power(n):
    return n in (1, 2, 4)


def exchange(make, axis, n):
    return [
        make(k) if k == 0 else lax.ppermute(make(k), axis, [(s, s ^ k) for s in range(n)])
        for k in range(n)
    ]


def per_device(n_out, n_inp, acts_rot, grads_rot, query_grads, query_acts, eigen, block_mask, order, segment_ids):
    rows, cols = eigen.shape
    queries = block_mask.shape[0]
    held = acts_rot.shape[0]
    tokens = order.shape[0]
    at_out, at_inp = lax.axis_index("out"), lax.axis_index("inp")
    unit = math.gcd(rows, BLOCK)
    tile = max(t for t in range(unit, 1024 + 1, unit) if rows % t == 0 and (t % BLOCK == 0 or t == rows))
    chunks = CHUNKS if (cols // BLOCK) % CHUNKS == 0 else 1
    width = cols // chunks
    col_blocks = width // BLOCK
    row_units, tile_units = rows // unit, tile // unit
    direct = is_small_power(n_out) and is_small_power(n_inp)
    t = jnp.arange(tokens, dtype=jnp.int32)

    if direct:
        near = exchange(
            lambda k: jnp.concatenate(
                [lax.dynamic_slice_in_dim(grads_rot, (at_out ^ k) * rows, rows, 1), acts_rot], axis=1
            ),
            "out", n_out,
        )
        shards = [
            exchange(lambda k: query_acts[:, :, c * width : (c + 1) * width], "out", n_out)
            for c in range(chunks)
        ]
        places = at_out ^ jnp.arange(n_out, dtype=jnp.int32)
    else:
        spread = lax.all_to_all(grads_rot[None], "out", split_axis=2, concat_axis=0, tiled=True)
        grads = lax.all_gather(spread, "inp", axis=1, tiled=True).reshape(-1, rows)
        whole_acts = lax.all_gather(acts_rot, ("out", "inp"), axis=0, tiled=True)
        acts = lax.dynamic_slice_in_dim(whole_acts, at_inp * cols, cols, 1)
        whole = lax.all_gather(query_acts, "out", axis=1, tiled=True)
        shards = [[whole[:, :, c * width : (c + 1) * width]] for c in range(chunks)]
        places = jnp.zeros((1,), jnp.int32)

    turned = turn(query_grads, tile)

    row_at = at_out * rows
    if rows % BLOCK == 0:
        band = lax.dynamic_slice_in_dim(block_mask, row_at // BLOCK, row_units, 1)
    else:
        band = jnp.take(block_mask, (row_at + unit * jnp.arange(row_units)) // BLOCK, axis=1)
    band = lax.dynamic_slice_in_dim(band, at_inp * (cols // BLOCK), cols // BLOCK, 2) > 0
    lists = [
        block_lists(band[:, :, c * col_blocks : (c + 1) * col_blocks], unit, tile_units, col_blocks)
        for c in range(chunks)
    ]

    if direct:
        near = jnp.concatenate(near, axis=0)
        both = exchange(
            lambda k: jnp.concatenate(
                [near[:, :rows], lax.dynamic_slice_in_dim(near, rows + (at_inp ^ k) * cols, cols, 1)],
                axis=1,
            ),
            "inp", n_inp,
        )
        both = jnp.concatenate(both, axis=0)
        grads, acts = both[:, :rows], both[:, rows:]
        per_inp = held * n_out
        from_inp = at_inp ^ (t // per_inp)
        from_out = at_out ^ (t % per_inp // held)
        arrived = (from_out * n_inp + from_inp) * held + t % held
    else:
        arrived = t
    position = jnp.sum(jnp.where(arrived[:, None] == t[None, :], order[None, :], 0), axis=1)
    sequence = jnp.sum(jnp.where(position[:, None] == t[None, :], segment_ids[None, :], 0), axis=1)
    reach = -(-(tokens + SEQS) // BLOCK) * BLOCK
    column = jnp.arange(reach, dtype=jnp.int32)[None, :]
    mapping = (
        (column == position[:, None]) | (column == tokens + sequence[:, None])
    ).astype(jnp.float32)

    scores = jnp.zeros((queries, reach), jnp.float32)
    for c in range(chunks):
        scores = score_part(
            lists[c], eigen, turned, shards[c], places, grads, acts, mapping, scores,
            unit, tile, c * width, width,
        )
    if direct:
        for axis, n in (("inp", n_inp), ("out", n_out)):
            k = 1
            while k < n:
                scores = scores + lax.ppermute(scores, axis, [(s, s ^ k) for s in range(n)])
                k *= 2
    else:
        scores = lax.psum(scores, ("out", "inp"))
    return scores[:, :tokens], scores[:, tokens : tokens + SEQS]


def solution(mesh):
    in_specs = (
        P(("groups", "out", "inp"), None),
        P(("groups", "out", "inp"), None),
        P("groups", None, "out"),
        P("groups", "out", "inp"),
        P("out", "inp"),
        P("groups", None, None),
        P("groups"),
        P("groups"),
    )
    out_specs = (P(None, "groups"), P("groups", None))
    return jax.shard_map(
        functools.partial(per_device, mesh.shape["out"], mesh.shape["inp"]),
        mesh=mesh, in_specs=in_specs, out_specs=out_specs, check_vma=False,
    )
```

```python
import functools
import math

import jax
import jax.numpy as jnp
from jax import lax
from jax.experimental import pallas as pl
from jax.experimental.pallas import tpu as pltpu
from jax.sharding import PartitionSpec as P


BLOCK = 128
SEQS = 4
UNROLL = 16
CHUNKS = 2
FLIGHT = 4

damping = 0.1


def score_kernel(
    unit, piece, first_col, shard_count,
    place_ref, end_ref, query_ref, row_ref, col_a_ref, col_b_ref, slot_a_ref, slot_b_ref,
    eigen_hbm, queries_hbm, grads_ref, acts_ref, map_ref, base_ref, *rest,
):
    shards, rest = rest[:shard_count], rest[shard_count:]
    out_ref, eigen_ref, queries_ref, weights_ref, grads_scr, sums_ref, sems = rest[:7]
    hold_a, hold_b = rest[7:][: UNROLL // 2], rest[7:][UNROLL // 2 :]
    rows, width = eigen_ref.shape
    queries = queries_hbm.shape[0]
    col_blocks = width // BLOCK
    pieces = rows // piece

    def copies(p):
        at = pl.ds(pl.multiple_of(p * piece, piece), piece)
        part = (slice(None), slice(None), at)
        if unit < BLOCK:
            part = (slice(None), pl.ds(p * (piece // unit), piece // unit))
        return (
            pltpu.make_async_copy(
                eigen_hbm.at[at, pl.ds(first_col, width)], eigen_ref.at[at, :], sems.at[0, p]
            ),
            pltpu.make_async_copy(queries_hbm.at[part], queries_ref.at[part], sems.at[1, p]),
        )

    for p in range(min(FLIGHT, pieces)):
        for copy in copies(p):
            copy.start()

    sums_ref[...] = jnp.zeros_like(sums_ref)
    weights_ref[queries * col_blocks] = jnp.zeros(weights_ref.shape[1:], weights_ref.dtype)
    for k, shard in enumerate(shards):
        held = shard.shape[1]
        place = pl.multiple_of(place_ref[k] * held, held)
        for q in range(queries):
            for c in range(col_blocks):
                weights_ref[q * col_blocks + c, pl.ds(place, held), :] = shard[
                    q, :, c * BLOCK : (c + 1) * BLOCK
                ]
    for r in range(rows // unit):
        grads_scr[r] = grads_ref[:, r * unit : (r + 1) * unit]
    for h in hold_b:
        h[...] = jnp.zeros_like(h)

    half = UNROLL // 2

    def outer_to(at, hold):
        rows_at = pl.ds(pl.multiple_of(row_ref[at] * unit, unit), unit)
        right = jnp.concatenate([weights_ref[slot_a_ref[at]], weights_ref[slot_b_ref[at]]], axis=1)
        query = query_ref[at]
        left = queries_ref[query, :, rows_at] if unit == BLOCK else queries_ref[query, row_ref[at]]
        outer = lax.dot_general(
            left,
            right,
            (((0,), (0,)), ((), ())),
            preferred_element_type=jnp.float32,
        )
        for h, col_ref in enumerate((col_a_ref, col_b_ref)):
            cols = pl.ds(pl.multiple_of(col_ref[at], BLOCK), BLOCK)
            scale = 1.0 / (eigen_ref[rows_at, cols].astype(jnp.float32) + damping)
            hold[:, h * BLOCK : (h + 1) * BLOCK] = (
                outer[:, h * BLOCK : (h + 1) * BLOCK] * scale
            ).astype(jnp.bfloat16)

    def add_part(at, hold):
        part = jnp.dot(grads_scr[row_ref[at]], hold[...], preferred_element_type=jnp.float32)
        sums_ref[slot_a_ref[at]] += part[:, :BLOCK]
        sums_ref[slot_b_ref[at]] += part[:, BLOCK:]

    def batch(k, before):
        start = k * UNROLL
        for s1, s2, at1, at2 in ((hold_a, hold_b, start, before), (hold_b, hold_a, start + half, start)):
            for u in range(half):
                outer_to(at1 + u, s1[u])
                add_part(at2 + u, s2[u])
        return start + half

    def one_piece(p, carry):
        k, before = carry
        for copy in copies(p):
            copy.wait()

        @pl.when(p + FLIGHT < pieces)
        def _():
            for copy in copies(p + FLIGHT):
                copy.start()

        end = end_ref[p]
        return end, lax.fori_loop(k, end, batch, before)

    idle = row_ref.shape[0] - UNROLL
    _, before = lax.fori_loop(0, pieces, one_piece, (jnp.int32(0), jnp.int32(idle)))
    for u in range(half):
        add_part(before + u, hold_b[u])

    for q in range(queries):
        total = sums_ref[q * col_blocks] * acts_ref[:, :BLOCK].astype(jnp.float32)
        for c in range(1, col_blocks):
            total += sums_ref[q * col_blocks + c] * acts_ref[
                :, c * BLOCK : (c + 1) * BLOCK
            ].astype(jnp.float32)
        score = jnp.sum(total, axis=1, keepdims=True)
        mapped = jnp.sum(score * map_ref[...], axis=0, keepdims=True)
        out_ref[q : q + 1, :] = base_ref[q : q + 1, :] + mapped


def block_lists(mask, unit, piece):
    queries, row_units, col_blocks = mask.shape
    half = (col_blocks + 1) // 2
    mask = mask.transpose(1, 0, 2)
    kept = mask.astype(jnp.int32)
    col = jnp.arange(col_blocks, dtype=jnp.int32)
    rank = jnp.sum(jnp.where(col[None, :] < col[:, None], kept[:, :, None, :], 0), axis=3)
    pair = jnp.arange(half, dtype=jnp.int32)[:, None]
    first = mask[:, :, None, :] & (rank[:, :, None, :] == 2 * pair)
    second = mask[:, :, None, :] & (rank[:, :, None, :] == 2 * pair + 1)
    col_a = jnp.sum(jnp.where(first, col, 0), axis=3)
    col_b = jnp.sum(jnp.where(second, col, 0), axis=3)
    count = jnp.sum(kept, axis=2)[:, :, None]
    has_a, has_b = count > 2 * pair[:, 0], count > 2 * pair[:, 0] + 1
    col_b = jnp.where(has_b, col_b, col_a)
    row = jnp.arange(row_units, dtype=jnp.int32)[:, None, None]
    query = jnp.arange(queries, dtype=jnp.int32)[None, :, None]
    code = (((query * row_units + row) * col_blocks + col_a) * col_blocks + col_b) * 2 + has_b.astype(jnp.int32)
    code, valid = (code + 1).reshape(-1), has_a.reshape(-1)
    entries = code.shape[0]
    length = -(-entries // UNROLL) * UNROLL + UNROLL
    at = jnp.arange(entries, dtype=jnp.int32)
    place = jnp.sum(jnp.where((at[None, :] < at[:, None]) & valid[None, :], 1, 0), axis=1)
    place = jnp.where(valid, place, -1)
    slots = jnp.arange(length, dtype=jnp.int32)
    packed = jnp.sum(jnp.where(place[None, :] == slots[:, None], code[None, :], 0), axis=1)
    there = packed > 0
    packed = jnp.maximum(packed - 1, 0)
    pieces = row_units * unit // piece
    upto = jnp.cumsum(jnp.sum(has_a.reshape(pieces, -1).astype(jnp.int32), axis=1))
    last = jnp.arange(pieces) == pieces - 1
    ends = jnp.where(last, -(-upto // UNROLL), upto // UNROLL).astype(jnp.int32)
    spare = queries * col_blocks
    has_b = there & (packed % 2 == 1)
    rest = packed // 2
    col_b = rest % col_blocks
    rest = rest // col_blocks
    col_a = rest % col_blocks
    rest = rest // col_blocks
    row = rest % row_units
    query = rest // row_units
    slot_a = jnp.where(there, query * col_blocks + col_a, spare)
    slot_b = jnp.where(has_b, query * col_blocks + col_b, spare)
    return [ends, query, row, col_a * BLOCK, col_b * BLOCK, slot_a, slot_b]


def score_part(lists, eigen, query_grads, shards, places, grads, acts, mapping, base, unit, piece, first_col, width):
    queries = query_grads.shape[0]
    rows = eigen.shape[0]
    query_tokens = shards[0].shape[1] * len(shards)
    tokens = grads.shape[0]
    col_blocks = width // BLOCK
    kernel = functools.partial(score_kernel, unit, piece, first_col, len(shards))
    vmem, hbm = pl.BlockSpec(memory_space=pltpu.VMEM), pl.BlockSpec(memory_space=pl.ANY)
    return pl.pallas_call(
        kernel,
        in_specs=[pl.BlockSpec(memory_space=pltpu.SMEM)] * 8 + [hbm, hbm] + [vmem] * (4 + len(shards)),
        out_specs=vmem,
        scratch_shapes=[
            pltpu.VMEM((rows, width), jnp.bfloat16),
            pltpu.VMEM(query_grads.shape, jnp.bfloat16),
            pltpu.VMEM((queries * col_blocks + 1, query_tokens, BLOCK), jnp.bfloat16),
            pltpu.VMEM((rows // unit, tokens, unit), jnp.bfloat16),
            pltpu.VMEM((queries * col_blocks + 1, tokens, BLOCK), jnp.float32),
            pltpu.SemaphoreType.DMA((2, rows // piece)),
            *[pltpu.VMEM((unit, 2 * BLOCK), jnp.bfloat16)] * UNROLL,
        ],
        out_shape=jax.ShapeDtypeStruct(base.shape, jnp.float32),
        compiler_params=pltpu.CompilerParams(vmem_limit_bytes=56 << 20),
    )(places, *lists, eigen, query_grads, grads, acts[:, first_col : first_col + width], mapping, base, *shards)


def is_small_power(n):
    return n in (1, 2, 4)


def exchange(make, axis, n):
    return [
        make(k) if k == 0 else lax.ppermute(make(k), axis, [(s, s ^ k) for s in range(n)])
        for k in range(n)
    ]


def per_device(n_out, n_inp, acts_rot, grads_rot, query_grads, query_acts, eigen, block_mask, order, segment_ids):
    rows, cols = eigen.shape
    queries = block_mask.shape[0]
    held = acts_rot.shape[0]
    tokens = order.shape[0]
    at_out, at_inp = lax.axis_index("out"), lax.axis_index("inp")
    unit = math.gcd(rows, BLOCK)
    tile = max(t for t in range(unit, 512 + 1, unit) if rows % t == 0 and (t % BLOCK == 0 or t == rows))
    chunks = CHUNKS if (cols // BLOCK) % CHUNKS == 0 else 1
    width = cols // chunks
    col_blocks = width // BLOCK
    row_units = rows // unit
    direct = is_small_power(n_out) and is_small_power(n_inp)
    t = jnp.arange(tokens, dtype=jnp.int32)

    if direct:
        near = exchange(
            lambda k: jnp.concatenate(
                [lax.dynamic_slice_in_dim(grads_rot, (at_out ^ k) * rows, rows, 1), acts_rot], axis=1
            ),
            "out", n_out,
        )
        shards = [
            exchange(lambda k: query_acts[:, :, c * width : (c + 1) * width], "out", n_out)
            for c in range(chunks)
        ]
        places = at_out ^ jnp.arange(n_out, dtype=jnp.int32)
    else:
        spread = lax.all_to_all(grads_rot[None], "out", split_axis=2, concat_axis=0, tiled=True)
        grads = lax.all_gather(spread, "inp", axis=1, tiled=True).reshape(-1, rows)
        whole_acts = lax.all_gather(acts_rot, ("out", "inp"), axis=0, tiled=True)
        acts = lax.dynamic_slice_in_dim(whole_acts, at_inp * cols, cols, 1)
        whole = lax.all_gather(query_acts, "out", axis=1, tiled=True)
        shards = [[whole[:, :, c * width : (c + 1) * width]] for c in range(chunks)]
        places = jnp.zeros((1,), jnp.int32)

    if unit < BLOCK:
        query_grads = query_grads.reshape(queries, -1, row_units, unit).transpose(0, 2, 1, 3)

    row_at = at_out * rows
    if rows % BLOCK == 0:
        band = lax.dynamic_slice_in_dim(block_mask, row_at // BLOCK, row_units, 1)
    else:
        band = jnp.take(block_mask, (row_at + unit * jnp.arange(row_units)) // BLOCK, axis=1)
    band = lax.dynamic_slice_in_dim(band, at_inp * (cols // BLOCK), cols // BLOCK, 2) > 0
    lists = [
        block_lists(band[:, :, c * col_blocks : (c + 1) * col_blocks], unit, tile)
        for c in range(chunks)
    ]

    if direct:
        near = jnp.concatenate(near, axis=0)
        both = exchange(
            lambda k: jnp.concatenate(
                [near[:, :rows], lax.dynamic_slice_in_dim(near, rows + (at_inp ^ k) * cols, cols, 1)],
                axis=1,
            ),
            "inp", n_inp,
        )
        both = jnp.concatenate(both, axis=0)
        grads, acts = both[:, :rows], both[:, rows:]
        per_inp = held * n_out
        from_inp = at_inp ^ (t // per_inp)
        from_out = at_out ^ (t % per_inp // held)
        arrived = (from_out * n_inp + from_inp) * held + t % held
    else:
        arrived = t
    position = jnp.sum(jnp.where(arrived[:, None] == t[None, :], order[None, :], 0), axis=1)
    sequence = jnp.sum(jnp.where(position[:, None] == t[None, :], segment_ids[None, :], 0), axis=1)
    reach = -(-(tokens + SEQS) // BLOCK) * BLOCK
    column = jnp.arange(reach, dtype=jnp.int32)[None, :]
    mapping = (
        (column == position[:, None]) | (column == tokens + sequence[:, None])
    ).astype(jnp.float32)

    scores = jnp.zeros((queries, reach), jnp.float32)
    for c in range(chunks):
        scores = score_part(
            lists[c], eigen, query_grads, shards[c], places, grads, acts, mapping, scores,
            unit, tile, c * width, width,
        )
    if direct:
        for axis, n in (("inp", n_inp), ("out", n_out)):
            k = 1
            while k < n:
                scores = scores + lax.ppermute(scores, axis, [(s, s ^ k) for s in range(n)])
                k *= 2
    else:
        scores = lax.psum(scores, ("out", "inp"))
    return scores[:, :tokens], scores[:, tokens : tokens + SEQS]


def solution(mesh):
    in_specs = (
        P(("groups", "out", "inp"), None),
        P(("groups", "out", "inp"), None),
        P("groups", None, "out"),
        P("groups", "out", "inp"),
        P("out", "inp"),
        P("groups", None, None),
        P("groups"),
        P("groups"),
    )
    out_specs = (P(None, "groups"), P("groups", None))
    return jax.shard_map(
        functools.partial(per_device, mesh.shape["out"], mesh.shape["inp"]),
        mesh=mesh, in_specs=in_specs, out_specs=out_specs, check_vma=False,
    )
```

```python
import functools
import math

import jax
import jax.numpy as jnp
from jax import lax
from jax.experimental import pallas as pl
from jax.experimental.pallas import tpu as pltpu
from jax.sharding import PartitionSpec as P


BLOCK = 128
SEQS = 4
UNROLL = 16
CHUNKS = 2
FLIGHT = 4
SLOT_BITS = 10

damping = 0.1


def score_kernel(
    unit, piece, first_col, shard_count, has_base,
    place_ref, end_ref, packed_ref,
    eigen_hbm, queries_hbm, near_ref, map_ref, *rest,
):
    if has_base:
        base_ref, rest = rest[0], rest[1:]
    shards, rest = rest[:shard_count], rest[shard_count:]
    out_ref, eigen_ref, queries_ref, weights_ref, grads_scr, sums_ref, sems = rest[:7]
    hold_a, hold_b = rest[7:][: UNROLL // 2], rest[7:][UNROLL // 2 :]
    rows, width = eigen_ref.shape
    queries = queries_hbm.shape[0]
    col_blocks = width // BLOCK
    pieces = rows // piece

    def copies(p):
        at = pl.ds(pl.multiple_of(p * piece, piece), piece)
        part = (slice(None), slice(None), at)
        if unit < BLOCK:
            part = (slice(None), pl.ds(p * (piece // unit), piece // unit))
        return (
            pltpu.make_async_copy(
                eigen_hbm.at[at, pl.ds(first_col, width)], eigen_ref.at[at, :], sems.at[0, p]
            ),
            pltpu.make_async_copy(queries_hbm.at[part], queries_ref.at[part], sems.at[1, p]),
        )

    for p in range(min(FLIGHT, pieces)):
        for copy in copies(p):
            copy.start()

    sums_ref[...] = jnp.zeros_like(sums_ref)
    weights_ref[queries * col_blocks] = jnp.zeros(weights_ref.shape[1:], weights_ref.dtype)
    for k, shard in enumerate(shards):
        held = shard.shape[1]
        place = pl.multiple_of(place_ref[k] * held, held)
        for q in range(queries):
            for c in range(col_blocks):
                weights_ref[q * col_blocks + c, pl.ds(place, held), :] = shard[
                    q, :, c * BLOCK : (c + 1) * BLOCK
                ]
    for r in range(rows // unit):
        grads_scr[r] = near_ref[:, r * unit : (r + 1) * unit]
    for h in hold_b:
        h[...] = jnp.zeros_like(h)

    half = UNROLL // 2

    def entry(at):
        code = packed_ref[at]
        low = (1 << SLOT_BITS) - 1
        return code >> 2 * SLOT_BITS, code >> SLOT_BITS & low, code & low

    def outer_to(at, hold):
        row, slot_a, slot_b = entry(at)
        query = jnp.minimum(lax.div(slot_a, col_blocks), queries - 1)
        rows_at = pl.ds(pl.multiple_of(row * unit, unit), unit)
        right = jnp.concatenate([weights_ref[slot_a], weights_ref[slot_b]], axis=1)
        left = queries_ref[query, :, rows_at] if unit == BLOCK else queries_ref[query, row]
        outer = lax.dot_general(
            left, right, (((0,), (0,)), ((), ())), preferred_element_type=jnp.float32
        )
        for h, slot in enumerate((slot_a, slot_b)):
            cols = pl.ds(pl.multiple_of(lax.rem(slot, col_blocks) * BLOCK, BLOCK), BLOCK)
            scale = 1.0 / (eigen_ref[rows_at, cols].astype(jnp.float32) + damping)
            hold[:, h * BLOCK : (h + 1) * BLOCK] = (
                outer[:, h * BLOCK : (h + 1) * BLOCK] * scale
            ).astype(jnp.bfloat16)

    def add_part(at, hold):
        row, slot_a, slot_b = entry(at)
        part = jnp.dot(grads_scr[row], hold[...], preferred_element_type=jnp.float32)
        sums_ref[slot_a] += part[:, :BLOCK]
        sums_ref[slot_b] += part[:, BLOCK:]

    def batch(k, before):
        start = k * UNROLL
        for s1, s2, at1, at2 in ((hold_a, hold_b, start, before), (hold_b, hold_a, start + half, start)):
            for u in range(half):
                outer_to(at1 + u, s1[u])
                add_part(at2 + u, s2[u])
        return start + half

    def one_piece(p, carry):
        k, before = carry
        for copy in copies(p):
            copy.wait()

        @pl.when(p + FLIGHT < pieces)
        def _():
            for copy in copies(p + FLIGHT):
                copy.start()

        end = end_ref[p]
        return end, lax.fori_loop(k, end, batch, before)

    idle = packed_ref.shape[0] - UNROLL
    _, before = lax.fori_loop(0, pieces, one_piece, (jnp.int32(0), jnp.int32(idle)))
    for u in range(half):
        add_part(before + u, hold_b[u])

    for q in range(queries):
        total = jnp.zeros(sums_ref.shape[1:], jnp.float32)
        for c in range(col_blocks):
            at = rows + first_col + c * BLOCK
            total += sums_ref[q * col_blocks + c] * near_ref[:, at : at + BLOCK].astype(jnp.float32)
        score = jnp.sum(total, axis=1, keepdims=True)
        mapped = jnp.sum(score * map_ref[...], axis=0, keepdims=True)
        out_ref[q : q + 1, :] = base_ref[q : q + 1, :] + mapped if has_base else mapped


def block_lists(mask, unit, piece, chunks):
    queries, row_units, _ = mask.shape
    mask = mask.reshape(queries, row_units, chunks, -1).transpose(2, 1, 0, 3)
    col_blocks = mask.shape[3]
    half = (col_blocks + 1) // 2
    kept = mask.astype(jnp.int32)
    col = jnp.arange(col_blocks, dtype=jnp.int32)
    rank = jnp.sum(jnp.where(col[None, :] < col[:, None], kept[..., None, :], 0), axis=-1)
    pair = jnp.arange(half, dtype=jnp.int32)
    hit = jnp.where(mask, rank, -1)[..., None, :]
    col_a = jnp.sum(jnp.where(hit == 2 * pair[:, None], col, 0), axis=-1)
    col_b = jnp.sum(jnp.where(hit == 2 * pair[:, None] + 1, col, 0), axis=-1)
    count = jnp.sum(kept, axis=-1)[..., None]
    has_a, has_b = count > 2 * pair, count > 2 * pair + 1
    row = jnp.arange(row_units, dtype=jnp.int32)[:, None, None]
    query = jnp.arange(queries, dtype=jnp.int32)[:, None]
    spare = queries * col_blocks
    slot_a = query * col_blocks + col_a
    slot_b = jnp.where(has_b, query * col_blocks + col_b, spare)
    code = ((row << SLOT_BITS | slot_a) << SLOT_BITS | slot_b) + 1
    code = jnp.where(has_a, code, 0).reshape(chunks, -1)
    entries = code.shape[1]
    length = -(-entries // UNROLL) * UNROLL + UNROLL
    at = jnp.arange(entries, dtype=jnp.int32)
    place = jnp.sum(((at[None, :] < at[:, None]) & (code > 0)[:, None, :]).astype(jnp.int32), axis=2)
    place = jnp.where(code > 0, place, -1)
    slots = jnp.arange(length, dtype=jnp.int32)
    packed = jnp.sum(jnp.where(place[:, None, :] == slots[:, None], code[:, None, :], 0), axis=2)
    packed = jnp.where(packed > 0, packed - 1, spare << SLOT_BITS | spare)
    pieces = row_units * unit // piece
    begin = jnp.arange(pieces, dtype=jnp.int32) * (entries // pieces)
    upto = jnp.sum(
        ((at[None, :] < begin[:, None] + entries // pieces) & (code > 0)[:, None, :]).astype(jnp.int32), axis=2
    )
    last = jnp.arange(pieces) == pieces - 1
    ends = jnp.where(last, -(-upto // UNROLL), upto // UNROLL).astype(jnp.int32)
    return ends, packed


def score_part(lists, eigen, query_grads, shards, places, near, mapping, base, unit, piece, first_col, width):
    queries = query_grads.shape[0]
    rows = eigen.shape[0]
    query_tokens = shards[0].shape[1] * len(shards)
    tokens = near.shape[0]
    col_blocks = width // BLOCK
    kernel = functools.partial(score_kernel, unit, piece, first_col, len(shards), base is not None)
    extra = [] if base is None else [base]
    vmem, hbm = pl.BlockSpec(memory_space=pltpu.VMEM), pl.BlockSpec(memory_space=pl.ANY)
    return pl.pallas_call(
        kernel,
        in_specs=[pl.BlockSpec(memory_space=pltpu.SMEM)] * 3 + [hbm, hbm] + [vmem] * (2 + len(extra) + len(shards)),
        out_specs=vmem,
        scratch_shapes=[
            pltpu.VMEM((rows, width), jnp.bfloat16),
            pltpu.VMEM(query_grads.shape, jnp.bfloat16),
            pltpu.VMEM((queries * col_blocks + 1, query_tokens, BLOCK), jnp.bfloat16),
            pltpu.VMEM((rows // unit, tokens, unit), jnp.bfloat16),
            pltpu.VMEM((queries * col_blocks + 1, tokens, BLOCK), jnp.float32),
            pltpu.SemaphoreType.DMA((2, rows // piece)),
            *[pltpu.VMEM((unit, 2 * BLOCK), jnp.bfloat16)] * UNROLL,
        ],
        out_shape=jax.ShapeDtypeStruct((queries, mapping.shape[1]), jnp.float32),
        compiler_params=pltpu.CompilerParams(vmem_limit_bytes=56 << 20),
    )(places, *lists, eigen, query_grads, near, mapping, *extra, *shards)


def is_small_power(n):
    return n in (1, 2, 4)


def exchange(make, axis, n):
    got = [make(0)]
    for k in range(1, n):
        payload = make(k)
        got.append(lax.ppermute(payload, axis, [(s, s ^ k) for s in range(n)]))
    return got


def scores_of(n_out, n_inp, acts_rot, grads_rot, query_grads, query_acts, eigen, block_mask, order, segment_ids):
    rows, cols = eigen.shape
    queries = block_mask.shape[0]
    held = acts_rot.shape[0]
    tokens = order.shape[0]
    at_out, at_inp = lax.axis_index("out"), lax.axis_index("inp")
    unit = math.gcd(rows, BLOCK)
    tile = max(t for t in range(unit, 512 + 1, unit) if rows % t == 0 and (t % BLOCK == 0 or t == rows))
    chunks = CHUNKS if (cols // BLOCK) % CHUNKS == 0 else 1
    width = cols // chunks
    row_units = rows // unit
    direct = is_small_power(n_out) and is_small_power(n_inp)
    t = jnp.arange(tokens, dtype=jnp.int32)

    if direct:
        near = exchange(
            lambda k: jnp.concatenate(
                [lax.dynamic_slice_in_dim(grads_rot, (at_out ^ k) * rows, rows, 1), acts_rot], axis=1
            ),
            "out", n_out,
        )
        shards = [
            exchange(lambda k: query_acts[:, :, c * width : (c + 1) * width], "out", n_out)
            for c in range(chunks)
        ]
        places = at_out ^ jnp.arange(n_out, dtype=jnp.int32)
    else:
        spread = lax.all_to_all(grads_rot[None], "out", split_axis=2, concat_axis=0, tiled=True)
        grads = lax.all_gather(spread, "inp", axis=1, tiled=True).reshape(-1, rows)
        whole_acts = lax.all_gather(acts_rot, ("out", "inp"), axis=0, tiled=True)
        acts = lax.dynamic_slice_in_dim(whole_acts, at_inp * cols, cols, 1)
        near = jnp.concatenate([grads, acts], axis=1)
        whole = lax.all_gather(query_acts, "out", axis=1, tiled=True)
        shards = [[whole[:, :, c * width : (c + 1) * width]] for c in range(chunks)]
        places = jnp.zeros((1,), jnp.int32)

    if unit < BLOCK:
        query_grads = query_grads.reshape(queries, -1, row_units, unit).transpose(0, 2, 1, 3)

    row_at = at_out * rows
    if rows % BLOCK == 0:
        band = lax.dynamic_slice_in_dim(block_mask, row_at // BLOCK, row_units, 1)
    else:
        band = jnp.take(block_mask, (row_at + unit * jnp.arange(row_units)) // BLOCK, axis=1)
    band = lax.dynamic_slice_in_dim(band, at_inp * (cols // BLOCK), cols // BLOCK, 2) > 0
    ends, packed = block_lists(band, unit, tile, chunks)

    if direct:
        near = jnp.concatenate(near, axis=0)
        both = exchange(
            lambda k: jnp.concatenate(
                [near[:, :rows], lax.dynamic_slice_in_dim(near, rows + (at_inp ^ k) * cols, cols, 1)],
                axis=1,
            ),
            "inp", n_inp,
        )
        near = jnp.concatenate(both, axis=0)
        per_inp = held * n_out
        from_inp = at_inp ^ (t // per_inp)
        from_out = at_out ^ (t % per_inp // held)
        arrived = (from_out * n_inp + from_inp) * held + t % held
    else:
        arrived = t
    position = jnp.sum(jnp.where(arrived[:, None] == t[None, :], order[None, :], 0), axis=1)
    sequence = jnp.sum(jnp.where(position[:, None] == t[None, :], segment_ids[None, :], 0), axis=1)
    reach = -(-(tokens + SEQS) // BLOCK) * BLOCK
    column = jnp.arange(reach, dtype=jnp.int32)[None, :]
    mapping = (
        (column == position[:, None]) | (column == tokens + sequence[:, None])
    ).astype(jnp.float32)

    scores = None
    for c in range(chunks):
        scores = score_part(
            (ends[c], packed[c]), eigen, query_grads, shards[c], places, near, mapping, scores,
            unit, tile, c * width, width,
        )
    if direct:
        for axis, n in (("inp", n_inp), ("out", n_out)):
            k = 1
            while k < n:
                scores = scores + lax.ppermute(scores, axis, [(s, s ^ k) for s in range(n)])
                k *= 2
    else:
        scores = lax.psum(scores, ("out", "inp"))
    return scores[:, :tokens], scores[:, tokens : tokens + SEQS]


def solution(mesh):
    in_specs = (
        P(("groups", "out", "inp"), None),
        P(("groups", "out", "inp"), None),
        P("groups", None, "out"),
        P("groups", "out", "inp"),
        P("out", "inp"),
        P("groups", None, None),
        P("groups"),
        P("groups"),
    )
    out_specs = (P(None, "groups"), P("groups", None))
    return jax.shard_map(
        functools.partial(scores_of, mesh.shape["out"], mesh.shape["inp"]),
        mesh=mesh, in_specs=in_specs, out_specs=out_specs, check_vma=False,
    )
```

```python
import functools
import math

import jax
import jax.numpy as jnp
from jax import lax
from jax.experimental import pallas as pl
from jax.experimental.pallas import tpu as pltpu
from jax.sharding import PartitionSpec as P


BLOCK = 128
SEQS = 4
UNROLL = 16
FLIGHT = 4
FIRST_SHARE = 9
SLOT_BITS = 10

damping = 0.1


def score_kernel(
    unit, piece, first_col, shard_count, has_base,
    place_ref, end_ref, packed_ref,
    eigen_hbm, queries_hbm, near_ref, map_ref, *rest,
):
    if has_base:
        base_ref, rest = rest[0], rest[1:]
    shards, rest = rest[:shard_count], rest[shard_count:]
    out_ref, eigen_ref, queries_ref, weights_ref, grads_scr, sums_ref, sems = rest[:7]
    hold_a, hold_b = rest[7:][: UNROLL // 2], rest[7:][UNROLL // 2 :]
    rows, width = eigen_ref.shape
    queries = queries_hbm.shape[0]
    col_blocks = width // BLOCK
    pieces = rows // piece

    def copies(p):
        at = pl.ds(pl.multiple_of(p * piece, piece), piece)
        part = (slice(None), slice(None), at)
        if unit < BLOCK:
            part = (slice(None), pl.ds(p * (piece // unit), piece // unit))
        return (
            pltpu.make_async_copy(
                eigen_hbm.at[at, pl.ds(first_col, width)], eigen_ref.at[at, :], sems.at[0, p]
            ),
            pltpu.make_async_copy(queries_hbm.at[part], queries_ref.at[part], sems.at[1, p]),
        )

    for p in range(min(FLIGHT, pieces)):
        for copy in copies(p):
            copy.start()

    sums_ref[...] = jnp.zeros_like(sums_ref)
    weights_ref[queries * col_blocks] = jnp.zeros(weights_ref.shape[1:], weights_ref.dtype)
    for k, shard in enumerate(shards):
        held = shard.shape[1]
        place = pl.multiple_of(place_ref[k] * held, held)
        for q in range(queries):
            for c in range(col_blocks):
                weights_ref[q * col_blocks + c, pl.ds(place, held), :] = shard[
                    q, :, c * BLOCK : (c + 1) * BLOCK
                ]
    for r in range(rows // unit):
        grads_scr[r] = near_ref[:, r * unit : (r + 1) * unit]
    for h in hold_b:
        h[...] = jnp.zeros_like(h)

    half = UNROLL // 2

    def entry(at):
        code = packed_ref[at]
        low = (1 << SLOT_BITS) - 1
        return code >> 2 * SLOT_BITS, code >> SLOT_BITS & low, code & low

    def outer_to(at, hold):
        row, slot_a, slot_b = entry(at)
        query = jnp.minimum(lax.div(slot_a, col_blocks), queries - 1)
        rows_at = pl.ds(pl.multiple_of(row * unit, unit), unit)
        right = jnp.concatenate([weights_ref[slot_a], weights_ref[slot_b]], axis=1)
        left = queries_ref[query, :, rows_at] if unit == BLOCK else queries_ref[query, row]
        outer = lax.dot_general(
            left, right, (((0,), (0,)), ((), ())), preferred_element_type=jnp.float32
        )
        for h, slot in enumerate((slot_a, slot_b)):
            cols = pl.ds(pl.multiple_of(lax.rem(slot, col_blocks) * BLOCK, BLOCK), BLOCK)
            scale = 1.0 / (eigen_ref[rows_at, cols].astype(jnp.float32) + damping)
            hold[:, h * BLOCK : (h + 1) * BLOCK] = (
                outer[:, h * BLOCK : (h + 1) * BLOCK] * scale
            ).astype(jnp.bfloat16)

    def add_part(at, hold):
        row, slot_a, slot_b = entry(at)
        part = jnp.dot(grads_scr[row], hold[...], preferred_element_type=jnp.float32)
        sums_ref[slot_a] += part[:, :BLOCK]
        sums_ref[slot_b] += part[:, BLOCK:]

    def batch(k, before):
        start = k * UNROLL
        for s1, s2, at1, at2 in ((hold_a, hold_b, start, before), (hold_b, hold_a, start + half, start)):
            for u in range(half):
                outer_to(at1 + u, s1[u])
                add_part(at2 + u, s2[u])
        return start + half

    def one_piece(p, carry):
        k, before = carry
        for copy in copies(p):
            copy.wait()

        @pl.when(p + FLIGHT < pieces)
        def _():
            for copy in copies(p + FLIGHT):
                copy.start()

        end = end_ref[p]
        return end, lax.fori_loop(k, end, batch, before)

    idle = packed_ref.shape[0] - UNROLL
    _, before = lax.fori_loop(0, pieces, one_piece, (jnp.int32(0), jnp.int32(idle)))
    for u in range(half):
        add_part(before + u, hold_b[u])

    for q in range(queries):
        total = jnp.zeros(sums_ref.shape[1:], jnp.float32)
        for c in range(col_blocks):
            at = rows + first_col + c * BLOCK
            total += sums_ref[q * col_blocks + c] * near_ref[:, at : at + BLOCK].astype(jnp.float32)
        score = jnp.sum(total, axis=1, keepdims=True)
        mapped = jnp.sum(score * map_ref[...], axis=0, keepdims=True)
        out_ref[q : q + 1, :] = base_ref[q : q + 1, :] + mapped if has_base else mapped


def block_lists(mask, unit, piece, blocks):
    queries, row_units, _ = mask.shape
    chunks, col_blocks = len(blocks), max(blocks)
    begins = [sum(blocks[:c]) for c in range(chunks)]
    mask = jnp.stack(
        [
            jnp.pad(mask[:, :, b : b + n], ((0, 0), (0, 0), (0, col_blocks - n)))
            for b, n in zip(begins, blocks)
        ]
    ).transpose(0, 2, 1, 3)
    half = (col_blocks + 1) // 2
    kept = mask.astype(jnp.int32)
    col = jnp.arange(col_blocks, dtype=jnp.int32)
    rank = jnp.sum(jnp.where(col[None, :] < col[:, None], kept[..., None, :], 0), axis=-1)
    pair = jnp.arange(half, dtype=jnp.int32)
    hit = jnp.where(mask, rank, -1)[..., None, :]
    col_a = jnp.sum(jnp.where(hit == 2 * pair[:, None], col, 0), axis=-1)
    col_b = jnp.sum(jnp.where(hit == 2 * pair[:, None] + 1, col, 0), axis=-1)
    count = jnp.sum(kept, axis=-1)[..., None]
    has_a, has_b = count > 2 * pair, count > 2 * pair + 1
    row = jnp.arange(row_units, dtype=jnp.int32)[:, None, None]
    query = jnp.arange(queries, dtype=jnp.int32)[:, None]
    stride = jnp.array(blocks, jnp.int32)[:, None, None, None]
    spare = queries * stride
    slot_a = query * stride + col_a
    slot_b = jnp.where(has_b, query * stride + col_b, spare)
    code = ((row << SLOT_BITS | slot_a) << SLOT_BITS | slot_b) + 1
    code = jnp.where(has_a, code, 0).reshape(chunks, -1)
    entries = code.shape[1]
    length = -(-entries // UNROLL) * UNROLL + UNROLL
    at = jnp.arange(entries, dtype=jnp.int32)
    place = jnp.sum(((at[None, :] < at[:, None]) & (code > 0)[:, None, :]).astype(jnp.int32), axis=2)
    place = jnp.where(code > 0, place, -1)
    slots = jnp.arange(length, dtype=jnp.int32)
    packed = jnp.sum(jnp.where(place[:, None, :] == slots[:, None], code[:, None, :], 0), axis=2)
    spare = spare[:, :, 0, 0]
    packed = jnp.where(packed > 0, packed - 1, spare << SLOT_BITS | spare)
    pieces = row_units * unit // piece
    begin = jnp.arange(pieces, dtype=jnp.int32) * (entries // pieces)
    upto = jnp.sum(
        ((at[None, :] < begin[:, None] + entries // pieces) & (code > 0)[:, None, :]).astype(jnp.int32), axis=2
    )
    last = jnp.arange(pieces) == pieces - 1
    ends = jnp.where(last, -(-upto // UNROLL), upto // UNROLL).astype(jnp.int32)
    return ends, packed


def score_part(lists, eigen, query_grads, shards, places, near, mapping, base, unit, piece, first_col, width):
    queries = query_grads.shape[0]
    rows = eigen.shape[0]
    query_tokens = shards[0].shape[1] * len(shards)
    tokens = near.shape[0]
    col_blocks = width // BLOCK
    kernel = functools.partial(score_kernel, unit, piece, first_col, len(shards), base is not None)
    extra = [] if base is None else [base]
    vmem, hbm = pl.BlockSpec(memory_space=pltpu.VMEM), pl.BlockSpec(memory_space=pl.ANY)
    return pl.pallas_call(
        kernel,
        in_specs=[pl.BlockSpec(memory_space=pltpu.SMEM)] * 3 + [hbm, hbm] + [vmem] * (2 + len(extra) + len(shards)),
        out_specs=vmem,
        scratch_shapes=[
            pltpu.VMEM((rows, width), jnp.bfloat16),
            pltpu.VMEM(query_grads.shape, jnp.bfloat16),
            pltpu.VMEM((queries * col_blocks + 1, query_tokens, BLOCK), jnp.bfloat16),
            pltpu.VMEM((rows // unit, tokens, unit), jnp.bfloat16),
            pltpu.VMEM((queries * col_blocks + 1, tokens, BLOCK), jnp.float32),
            pltpu.SemaphoreType.DMA((2, rows // piece)),
            *[pltpu.VMEM((unit, 2 * BLOCK), jnp.bfloat16)] * UNROLL,
        ],
        out_shape=jax.ShapeDtypeStruct((queries, mapping.shape[1]), jnp.float32),
        compiler_params=pltpu.CompilerParams(vmem_limit_bytes=56 << 20),
    )(places, *lists, eigen, query_grads, near, mapping, *extra, *shards)


def is_small_power(n):
    return n in (1, 2, 4)


def exchange(make, axis, n):
    got = [make(0)]
    for k in range(1, n):
        payload = make(k)
        got.append(lax.ppermute(payload, axis, [(s, s ^ k) for s in range(n)]))
    return got


def scores_of(n_out, n_inp, acts_rot, grads_rot, query_grads, query_acts, eigen, block_mask, order, segment_ids):
    rows, cols = eigen.shape
    queries = block_mask.shape[0]
    held = acts_rot.shape[0]
    tokens = order.shape[0]
    at_out, at_inp = lax.axis_index("out"), lax.axis_index("inp")
    unit = math.gcd(rows, BLOCK)
    tile = max(t for t in range(unit, 512 + 1, unit) if rows % t == 0 and (t % BLOCK == 0 or t == rows))
    first = cols // BLOCK * FIRST_SHARE // 16 * BLOCK
    widths = (first, cols - first)
    begins = (0, first)
    chunks = len(widths)
    row_units = rows // unit
    direct = is_small_power(n_out) and is_small_power(n_inp)
    t = jnp.arange(tokens, dtype=jnp.int32)

    if direct:
        near = exchange(
            lambda k: jnp.concatenate(
                [lax.dynamic_slice_in_dim(grads_rot, (at_out ^ k) * rows, rows, 1), acts_rot], axis=1
            ),
            "out", n_out,
        )
        shards = [
            exchange(lambda k: query_acts[:, :, begins[c] : begins[c] + widths[c]], "out", n_out)
            for c in range(chunks)
        ]
        places = at_out ^ jnp.arange(n_out, dtype=jnp.int32)
    else:
        spread = lax.all_to_all(grads_rot[None], "out", split_axis=2, concat_axis=0, tiled=True)
        grads = lax.all_gather(spread, "inp", axis=1, tiled=True).reshape(-1, rows)
        whole_acts = lax.all_gather(acts_rot, ("out", "inp"), axis=0, tiled=True)
        acts = lax.dynamic_slice_in_dim(whole_acts, at_inp * cols, cols, 1)
        near = jnp.concatenate([grads, acts], axis=1)
        whole = lax.all_gather(query_acts, "out", axis=1, tiled=True)
        shards = [[whole[:, :, begins[c] : begins[c] + widths[c]]] for c in range(chunks)]
        places = jnp.zeros((1,), jnp.int32)

    if direct:
        near = jnp.concatenate(near, axis=0)
        near, block_mask = lax.optimization_barrier((near, block_mask))
    if unit < BLOCK:
        query_grads = query_grads.reshape(queries, -1, row_units, unit).transpose(0, 2, 1, 3)

    row_at = at_out * rows
    if rows % BLOCK == 0:
        band = lax.dynamic_slice_in_dim(block_mask, row_at // BLOCK, row_units, 1)
    else:
        band = jnp.take(block_mask, (row_at + unit * jnp.arange(row_units)) // BLOCK, axis=1)
    band = lax.dynamic_slice_in_dim(band, at_inp * (cols // BLOCK), cols // BLOCK, 2) > 0
    ends, packed = block_lists(band, unit, tile, [w // BLOCK for w in widths])

    if direct:
        both = exchange(
            lambda k: jnp.concatenate(
                [near[:, :rows], lax.dynamic_slice_in_dim(near, rows + (at_inp ^ k) * cols, cols, 1)],
                axis=1,
            ),
            "inp", n_inp,
        )
        near = jnp.concatenate(both, axis=0)
        per_inp = held * n_out
        from_inp = at_inp ^ (t // per_inp)
        from_out = at_out ^ (t % per_inp // held)
        arrived = (from_out * n_inp + from_inp) * held + t % held
    else:
        arrived = t
    position = jnp.sum(jnp.where(arrived[:, None] == t[None, :], order[None, :], 0), axis=1)
    sequence = jnp.sum(jnp.where(position[:, None] == t[None, :], segment_ids[None, :], 0), axis=1)
    reach = -(-(tokens + SEQS) // BLOCK) * BLOCK
    column = jnp.arange(reach, dtype=jnp.int32)[None, :]
    mapping = (
        (column == position[:, None]) | (column == tokens + sequence[:, None])
    ).astype(jnp.float32)

    scores = None
    for c in range(chunks):
        scores = score_part(
            (ends[c], packed[c]), eigen, query_grads, shards[c], places, near, mapping, scores,
            unit, tile, begins[c], widths[c],
        )
    if direct:
        for axis, n in (("inp", n_inp), ("out", n_out)):
            k = 1
            while k < n:
                scores = scores + lax.ppermute(scores, axis, [(s, s ^ k) for s in range(n)])
                k *= 2
    else:
        scores = lax.psum(scores, ("out", "inp"))
    return scores[:, :tokens], scores[:, tokens : tokens + SEQS]


def solution(mesh):
    in_specs = (
        P(("groups", "out", "inp"), None),
        P(("groups", "out", "inp"), None),
        P("groups", None, "out"),
        P("groups", "out", "inp"),
        P("out", "inp"),
        P("groups", None, None),
        P("groups"),
        P("groups"),
    )
    out_specs = (P(None, "groups"), P("groups", None))
    return jax.shard_map(
        functools.partial(scores_of, mesh.shape["out"], mesh.shape["inp"]),
        mesh=mesh, in_specs=in_specs, out_specs=out_specs, check_vma=False,
    )
```

```python
import functools
import math

import jax
import jax.numpy as jnp
from jax import lax
from jax.experimental import pallas as pl
from jax.experimental.pallas import tpu as pltpu
from jax.sharding import PartitionSpec as P


BLOCK = 128
SEQS = 4
UNROLL = 24
FLIGHT = 4
FIRST_SHARE = 8
SLOT_BITS = 10

damping = 0.1


def score_kernel(
    unit, piece, first_col, shard_count, has_base,
    place_ref, end_ref, packed_ref,
    eigen_hbm, queries_hbm, near_ref, map_ref, *rest,
):
    if has_base:
        base_ref, rest = rest[0], rest[1:]
    shards, rest = rest[:shard_count], rest[shard_count:]
    out_ref, eigen_ref, queries_ref, weights_ref, grads_scr, sums_ref, sems = rest[:7]
    hold_a, hold_b = rest[7:][: UNROLL // 2], rest[7:][UNROLL // 2 :]
    rows, width = eigen_ref.shape
    queries = queries_hbm.shape[0]
    col_blocks = width // BLOCK
    pieces = rows // piece

    def copies(p):
        at = pl.ds(pl.multiple_of(p * piece, piece), piece)
        part = (slice(None), slice(None), at)
        if unit < BLOCK:
            part = (slice(None), pl.ds(p * (piece // unit), piece // unit))
        return (
            pltpu.make_async_copy(
                eigen_hbm.at[at, pl.ds(first_col, width)], eigen_ref.at[at, :], sems.at[0, p]
            ),
            pltpu.make_async_copy(queries_hbm.at[part], queries_ref.at[part], sems.at[1, p]),
        )

    for p in range(min(FLIGHT, pieces)):
        for copy in copies(p):
            copy.start()

    sums_ref[...] = jnp.zeros_like(sums_ref)
    weights_ref[queries * col_blocks] = jnp.zeros(weights_ref.shape[1:], weights_ref.dtype)
    for k, shard in enumerate(shards):
        held = shard.shape[1]
        place = pl.multiple_of(place_ref[k] * held, held)
        for q in range(queries):
            for c in range(col_blocks):
                weights_ref[q * col_blocks + c, pl.ds(place, held), :] = shard[
                    q, :, c * BLOCK : (c + 1) * BLOCK
                ]
    for r in range(rows // unit):
        grads_scr[r] = near_ref[:, r * unit : (r + 1) * unit]
    for h in hold_b:
        h[...] = jnp.zeros_like(h)

    half = UNROLL // 2

    def entry(at):
        code = packed_ref[at]
        low = (1 << SLOT_BITS) - 1
        return code >> 2 * SLOT_BITS, code >> SLOT_BITS & low, code & low

    def outer_to(at, hold):
        row, slot_a, slot_b = entry(at)
        query = jnp.minimum(lax.div(slot_a, col_blocks), queries - 1)
        rows_at = pl.ds(pl.multiple_of(row * unit, unit), unit)
        left = queries_ref[query, :, rows_at] if unit == BLOCK else queries_ref[query, row]
        right = jnp.concatenate(
            [weights_ref[slot, : left.shape[0], :] for slot in (slot_a, slot_b)], axis=1
        )
        outer = lax.dot_general(
            left, right, (((0,), (0,)), ((), ())), preferred_element_type=jnp.float32
        )
        for h, slot in enumerate((slot_a, slot_b)):
            cols = pl.ds(pl.multiple_of(lax.rem(slot, col_blocks) * BLOCK, BLOCK), BLOCK)
            scale = 1.0 / (eigen_ref[rows_at, cols].astype(jnp.float32) + damping)
            hold[h] = (
                outer[:, h * BLOCK : (h + 1) * BLOCK] * scale
            ).astype(jnp.bfloat16)

    def add_part(at, hold):
        row, slot_a, slot_b = entry(at)
        part = jnp.dot(grads_scr[row], jnp.concatenate([hold[0], hold[1]], axis=1), preferred_element_type=jnp.float32)
        sums_ref[slot_a] += part[:, :BLOCK]
        sums_ref[slot_b] += part[:, BLOCK:]

    def batch(k, before):
        start = k * UNROLL
        for s1, s2, at1, at2 in ((hold_a, hold_b, start, before), (hold_b, hold_a, start + half, start)):
            for u in range(half):
                outer_to(at1 + u, s1[u])
                add_part(at2 + u, s2[u])
        return start + half

    def one_piece(p, carry):
        k, before = carry
        for copy in copies(p):
            copy.wait()

        @pl.when(p + FLIGHT < pieces)
        def _():
            for copy in copies(p + FLIGHT):
                copy.start()

        end = end_ref[p]
        return end, lax.fori_loop(k, end, batch, before)

    idle = packed_ref.shape[0] - UNROLL
    _, before = lax.fori_loop(0, pieces, one_piece, (jnp.int32(0), jnp.int32(idle)))
    for u in range(half):
        add_part(before + u, hold_b[u])

    for q in range(queries):
        total = jnp.zeros(sums_ref.shape[1:], jnp.float32)
        for c in range(col_blocks):
            at = rows + first_col + c * BLOCK
            total += sums_ref[q * col_blocks + c] * near_ref[:, at : at + BLOCK].astype(jnp.float32)
        score = jnp.sum(total, axis=1, keepdims=True)
        mapped = jnp.sum(score * map_ref[...], axis=0, keepdims=True)
        out_ref[q : q + 1, :] = base_ref[q : q + 1, :] + mapped if has_base else mapped


def block_lists(mask, unit, piece, blocks):
    queries, row_units, _ = mask.shape
    chunks, col_blocks = len(blocks), max(blocks)
    begins = [sum(blocks[:c]) for c in range(chunks)]
    mask = jnp.stack(
        [
            jnp.pad(mask[:, :, b : b + n], ((0, 0), (0, 0), (0, col_blocks - n)))
            for b, n in zip(begins, blocks)
        ]
    ).transpose(0, 2, 1, 3)
    half = (col_blocks + 1) // 2
    kept = mask.astype(jnp.int32)
    col = jnp.arange(col_blocks, dtype=jnp.int32)
    rank = jnp.sum(jnp.where(col[None, :] < col[:, None], kept[..., None, :], 0), axis=-1)
    pair = jnp.arange(half, dtype=jnp.int32)
    hit = jnp.where(mask, rank, -1)[..., None, :]
    col_a = jnp.sum(jnp.where(hit == 2 * pair[:, None], col, 0), axis=-1)
    col_b = jnp.sum(jnp.where(hit == 2 * pair[:, None] + 1, col, 0), axis=-1)
    count = jnp.sum(kept, axis=-1)[..., None]
    has_a, has_b = count > 2 * pair, count > 2 * pair + 1
    row = jnp.arange(row_units, dtype=jnp.int32)[:, None, None]
    query = jnp.arange(queries, dtype=jnp.int32)[:, None]
    stride = jnp.array(blocks, jnp.int32)[:, None, None, None]
    spare = queries * stride
    slot_a = query * stride + col_a
    slot_b = jnp.where(has_b, query * stride + col_b, spare)
    code = ((row << SLOT_BITS | slot_a) << SLOT_BITS | slot_b) + 1
    code = jnp.where(has_a, code, 0).reshape(chunks, -1)
    entries = code.shape[1]
    length = -(-entries // UNROLL) * UNROLL + UNROLL
    at = jnp.arange(entries, dtype=jnp.int32)
    place = jnp.sum(((at[None, :] < at[:, None]) & (code > 0)[:, None, :]).astype(jnp.int32), axis=2)
    place = jnp.where(code > 0, place, -1)
    slots = jnp.arange(length, dtype=jnp.int32)
    packed = jnp.sum(jnp.where(place[:, None, :] == slots[:, None], code[:, None, :], 0), axis=2)
    spare = spare[:, :, 0, 0]
    packed = jnp.where(packed > 0, packed - 1, spare << SLOT_BITS | spare)
    pieces = row_units * unit // piece
    begin = jnp.arange(pieces, dtype=jnp.int32) * (entries // pieces)
    upto = jnp.sum(
        ((at[None, :] < begin[:, None] + entries // pieces) & (code > 0)[:, None, :]).astype(jnp.int32), axis=2
    )
    last = jnp.arange(pieces) == pieces - 1
    ends = jnp.where(last, -(-upto // UNROLL), upto // UNROLL).astype(jnp.int32)
    return ends, packed


def score_part(lists, eigen, query_grads, shards, places, near, mapping, base, unit, piece, first_col, width):
    queries = query_grads.shape[0]
    rows = eigen.shape[0]
    token_space = shards[0].shape[1] * len(shards)
    tokens = near.shape[0]
    col_blocks = width // BLOCK
    kernel = functools.partial(score_kernel, unit, piece, first_col, len(shards), base is not None)
    extra = [] if base is None else [base]
    vmem, hbm = pl.BlockSpec(memory_space=pltpu.VMEM), pl.BlockSpec(memory_space=pl.ANY)
    return pl.pallas_call(
        kernel,
        in_specs=[pl.BlockSpec(memory_space=pltpu.SMEM)] * 3 + [hbm, hbm] + [vmem] * (2 + len(extra) + len(shards)),
        out_specs=vmem,
        scratch_shapes=[
            pltpu.VMEM((rows, width), jnp.bfloat16),
            pltpu.VMEM(query_grads.shape, jnp.bfloat16),
            pltpu.VMEM((queries * col_blocks + 1, token_space, BLOCK), jnp.bfloat16),
            pltpu.VMEM((rows // unit, tokens, unit), jnp.bfloat16),
            pltpu.VMEM((queries * col_blocks + 1, tokens, BLOCK), jnp.float32),
            pltpu.SemaphoreType.DMA((2, rows // piece)),
            *[pltpu.VMEM((2, unit, BLOCK), jnp.bfloat16)] * UNROLL,
        ],
        out_shape=jax.ShapeDtypeStruct((queries, mapping.shape[1]), jnp.float32),
        compiler_params=pltpu.CompilerParams(vmem_limit_bytes=56 << 20),
    )(places, *lists, eigen, query_grads, near, mapping, *extra, *shards)


def is_small_power(n):
    return n in (1, 2, 4)


def exchange(make, axis, n):
    got = [make(0)]
    for k in range(1, n):
        payload = make(k)
        got.append(lax.ppermute(payload, axis, [(s, s ^ k) for s in range(n)]))
    return got


def relay_exchange(mine, axis):
    far = lax.ppermute(mine, axis, [(0, 2), (2, 0), (1, 3), (3, 1)])
    near = lax.ppermute(mine, axis, [(0, 1), (1, 0), (2, 3), (3, 2)])
    middle = lax.ppermute(mine, axis, [(1, 2), (2, 1)])
    ends = lax.ppermute(far, axis, [(2, 3), (1, 0)])
    return [mine, near, far, middle, ends]


def scores_of(n_out, n_inp, acts_rot, grads_rot, query_grads, query_acts, eigen, block_mask, order, segment_ids):
    rows, cols = eigen.shape
    queries = block_mask.shape[0]
    held = acts_rot.shape[0]
    tokens = order.shape[0]
    at_out, at_inp = lax.axis_index("out"), lax.axis_index("inp")
    unit = math.gcd(rows, BLOCK)
    tile = max(t for t in range(unit, 512 + 1, unit) if rows % t == 0 and (t % BLOCK == 0 or t == rows))
    first = cols // BLOCK * FIRST_SHARE // 16 * BLOCK
    widths = (first, cols - first)
    begins = (0, first)
    chunks = len(widths)
    row_units = rows // unit
    direct = is_small_power(n_out) and is_small_power(n_inp)
    t = jnp.arange(tokens, dtype=jnp.int32)

    if direct:
        near = exchange(
            lambda k: jnp.concatenate(
                [lax.dynamic_slice_in_dim(grads_rot, (at_out ^ k) * rows, rows, 1), acts_rot], axis=1
            ),
            "out", n_out,
        )
        sent = [query_acts[:, :, b : b + w] for b, w in zip(begins, widths)]
        places = [at_out ^ jnp.arange(n_out, dtype=jnp.int32)] * chunks
        if n_out == 4:
            shards = [relay_exchange(sent[0], "out")]
            other = at_out ^ 3
            inner = (at_out == 1) | (at_out == 2)
            places[0] = jnp.stack(
                [at_out, at_out ^ 1, at_out ^ 2, jnp.where(inner, other, 4), jnp.where(inner, 4, other)]
            ).astype(jnp.int32)
        else:
            shards = [exchange(lambda k: sent[0], "out", n_out)]
        shards.append(exchange(lambda k: sent[1], "out", n_out))
    else:
        spread = lax.all_to_all(grads_rot[None], "out", split_axis=2, concat_axis=0, tiled=True)
        grads = lax.all_gather(spread, "inp", axis=1, tiled=True).reshape(-1, rows)
        whole_acts = lax.all_gather(acts_rot, ("out", "inp"), axis=0, tiled=True)
        acts = lax.dynamic_slice_in_dim(whole_acts, at_inp * cols, cols, 1)
        near = jnp.concatenate([grads, acts], axis=1)
        whole = lax.all_gather(query_acts, "out", axis=1, tiled=True)
        shards = [[whole[:, :, begins[c] : begins[c] + widths[c]]] for c in range(chunks)]
        places = [jnp.zeros((1,), jnp.int32)] * chunks

    if direct:
        near = jnp.concatenate(near, axis=0)
        near, block_mask = lax.optimization_barrier((near, block_mask))
    if unit < BLOCK:
        query_grads = query_grads.reshape(queries, -1, row_units, unit).transpose(0, 2, 1, 3)

    row_at = at_out * rows
    if rows % BLOCK == 0:
        band = lax.dynamic_slice_in_dim(block_mask, row_at // BLOCK, row_units, 1)
    else:
        band = jnp.take(block_mask, (row_at + unit * jnp.arange(row_units)) // BLOCK, axis=1)
    band = lax.dynamic_slice_in_dim(band, at_inp * (cols // BLOCK), cols // BLOCK, 2) > 0
    ends, packed = block_lists(band, unit, tile, [w // BLOCK for w in widths])

    if direct:
        both = exchange(
            lambda k: jnp.concatenate(
                [near[:, :rows], lax.dynamic_slice_in_dim(near, rows + (at_inp ^ k) * cols, cols, 1)],
                axis=1,
            ),
            "inp", n_inp,
        )
        near = jnp.concatenate(both, axis=0)
        per_inp = held * n_out
        from_inp = at_inp ^ (t // per_inp)
        from_out = at_out ^ (t % per_inp // held)
        arrived = (from_out * n_inp + from_inp) * held + t % held
    else:
        arrived = t
    position = jnp.sum(jnp.where(arrived[:, None] == t[None, :], order[None, :], 0), axis=1)
    sequence = jnp.sum(jnp.where(position[:, None] == t[None, :], segment_ids[None, :], 0), axis=1)
    reach = -(-(tokens + SEQS) // BLOCK) * BLOCK
    column = jnp.arange(reach, dtype=jnp.int32)[None, :]
    mapping = (
        (column == position[:, None]) | (column == tokens + sequence[:, None])
    ).astype(jnp.float32)

    scores = None
    for c in range(chunks):
        scores = score_part(
            (ends[c], packed[c]), eigen, query_grads, shards[c], places[c], near, mapping, scores,
            unit, tile, begins[c], widths[c],
        )
    if direct:
        for axis, n in (("inp", n_inp), ("out", n_out)):
            k = 1
            while k < n:
                scores = scores + lax.ppermute(scores, axis, [(s, s ^ k) for s in range(n)])
                k *= 2
    else:
        scores = lax.psum(scores, ("out", "inp"))
    return scores[:, :tokens], scores[:, tokens : tokens + SEQS]


def solution(mesh):
    in_specs = (
        P(("groups", "out", "inp"), None),
        P(("groups", "out", "inp"), None),
        P("groups", None, "out"),
        P("groups", "out", "inp"),
        P("out", "inp"),
        P("groups", None, None),
        P("groups"),
        P("groups"),
    )
    out_specs = (P(None, "groups"), P("groups", None))
    return jax.shard_map(
        functools.partial(scores_of, mesh.shape["out"], mesh.shape["inp"]),
        mesh=mesh, in_specs=in_specs, out_specs=out_specs, check_vma=False,
    )
```

```python
import functools
import math

import jax
import jax.numpy as jnp
from jax import lax
from jax.experimental import pallas as pl
from jax.experimental.pallas import tpu as pltpu
from jax.sharding import PartitionSpec as P


BLOCK = 128
SEQS = 4
UNROLL = 16
FLIGHT = 4
FIRST_SHARE = 9
SLOT_BITS = 10

damping = 0.1


def score_kernel(
    unit, piece, first_col, shard_count, has_base,
    place_ref, end_ref, packed_ref,
    eigen_hbm, queries_hbm, near_ref, map_ref, *rest,
):
    if has_base:
        base_ref, rest = rest[0], rest[1:]
    shards, rest = rest[:shard_count], rest[shard_count:]
    out_ref, eigen_ref, queries_ref, weights_ref, grads_scr, sums_ref, sems = rest[:7]
    hold_a, hold_b = rest[7:][: UNROLL // 2], rest[7:][UNROLL // 2 :]
    rows, width = eigen_ref.shape
    queries = queries_hbm.shape[0]
    col_blocks = width // BLOCK
    pieces = rows // piece

    def copies(p):
        at = pl.ds(pl.multiple_of(p * piece, piece), piece)
        part = (slice(None), slice(None), at)
        if unit < BLOCK:
            part = (slice(None), pl.ds(p * (piece // unit), piece // unit))
        return (
            pltpu.make_async_copy(
                eigen_hbm.at[at, pl.ds(first_col, width)], eigen_ref.at[at, :], sems.at[0, p]
            ),
            pltpu.make_async_copy(queries_hbm.at[part], queries_ref.at[part], sems.at[1, p]),
        )

    for p in range(min(FLIGHT, pieces)):
        for copy in copies(p):
            copy.start()

    sums_ref[...] = jnp.zeros_like(sums_ref)
    weights_ref[queries * col_blocks] = jnp.zeros(weights_ref.shape[1:], weights_ref.dtype)
    for k, shard in enumerate(shards):
        held = shard.shape[1]
        place = pl.multiple_of(place_ref[k] * held, held)
        for q in range(queries):
            for c in range(col_blocks):
                weights_ref[q * col_blocks + c, pl.ds(place, held), :] = shard[
                    q, :, c * BLOCK : (c + 1) * BLOCK
                ]
    for r in range(rows // unit):
        grads_scr[r] = near_ref[:, r * unit : (r + 1) * unit]
    for h in hold_b:
        h[...] = jnp.zeros_like(h)

    half = UNROLL // 2

    def entry(at):
        code = packed_ref[at]
        low = (1 << SLOT_BITS) - 1
        return code >> 2 * SLOT_BITS, code >> SLOT_BITS & low, code & low

    def outer_to(at, hold):
        row, slot_a, slot_b = entry(at)
        query = jnp.minimum(lax.div(slot_a, col_blocks), queries - 1)
        rows_at = pl.ds(pl.multiple_of(row * unit, unit), unit)
        left = queries_ref[query, :, rows_at] if unit == BLOCK else queries_ref[query, row]
        right = jnp.concatenate(
            [weights_ref[slot, : left.shape[0], :] for slot in (slot_a, slot_b)], axis=1
        )
        outer = lax.dot_general(
            left, right, (((0,), (0,)), ((), ())), preferred_element_type=jnp.float32
        )
        for h, slot in enumerate((slot_a, slot_b)):
            cols = pl.ds(pl.multiple_of(lax.rem(slot, col_blocks) * BLOCK, BLOCK), BLOCK)
            scale = 1.0 / (eigen_ref[rows_at, cols].astype(jnp.float32) + damping)
            hold[h] = (
                outer[:, h * BLOCK : (h + 1) * BLOCK] * scale
            ).astype(jnp.bfloat16)

    def add_part(at, hold):
        row, slot_a, slot_b = entry(at)
        part = jnp.dot(grads_scr[row], jnp.concatenate([hold[0], hold[1]], axis=1), preferred_element_type=jnp.float32)
        sums_ref[slot_a] += part[:, :BLOCK]
        sums_ref[slot_b] += part[:, BLOCK:]

    def batch(k, before):
        start = k * UNROLL
        for s1, s2, at1, at2 in ((hold_a, hold_b, start, before), (hold_b, hold_a, start + half, start)):
            for u in range(half):
                outer_to(at1 + u, s1[u])
                add_part(at2 + u, s2[u])
        return start + half

    def one_piece(p, carry):
        k, before = carry
        for copy in copies(p):
            copy.wait()

        @pl.when(p + FLIGHT < pieces)
        def _():
            for copy in copies(p + FLIGHT):
                copy.start()

        end = end_ref[p]
        return end, lax.fori_loop(k, end, batch, before)

    idle = packed_ref.shape[0] - UNROLL
    _, before = lax.fori_loop(0, pieces, one_piece, (jnp.int32(0), jnp.int32(idle)))
    for u in range(half):
        add_part(before + u, hold_b[u])

    for q in range(queries):
        total = jnp.zeros(sums_ref.shape[1:], jnp.float32)
        for c in range(col_blocks):
            at = rows + first_col + c * BLOCK
            total += sums_ref[q * col_blocks + c] * near_ref[:, at : at + BLOCK].astype(jnp.float32)
        score = jnp.sum(total, axis=1, keepdims=True)
        mapped = jnp.sum(score * map_ref[...], axis=0, keepdims=True)
        out_ref[q : q + 1, :] = base_ref[q : q + 1, :] + mapped if has_base else mapped


def block_lists(mask, unit, piece, blocks):
    queries, row_units, _ = mask.shape
    chunks, col_blocks = len(blocks), max(blocks)
    begins = [sum(blocks[:c]) for c in range(chunks)]
    mask = jnp.stack(
        [
            jnp.pad(mask[:, :, b : b + n], ((0, 0), (0, 0), (0, col_blocks - n)))
            for b, n in zip(begins, blocks)
        ]
    ).transpose(0, 2, 1, 3)
    half = (col_blocks + 1) // 2
    kept = mask.astype(jnp.int32)
    col = jnp.arange(col_blocks, dtype=jnp.int32)
    rank = jnp.sum(jnp.where(col[None, :] < col[:, None], kept[..., None, :], 0), axis=-1)
    pair = jnp.arange(half, dtype=jnp.int32)
    hit = jnp.where(mask, rank, -1)[..., None, :]
    col_a = jnp.sum(jnp.where(hit == 2 * pair[:, None], col, 0), axis=-1)
    col_b = jnp.sum(jnp.where(hit == 2 * pair[:, None] + 1, col, 0), axis=-1)
    count = jnp.sum(kept, axis=-1)[..., None]
    has_a, has_b = count > 2 * pair, count > 2 * pair + 1
    row = jnp.arange(row_units, dtype=jnp.int32)[:, None, None]
    query = jnp.arange(queries, dtype=jnp.int32)[:, None]
    stride = jnp.array(blocks, jnp.int32)[:, None, None, None]
    spare = queries * stride
    slot_a = query * stride + col_a
    slot_b = jnp.where(has_b, query * stride + col_b, spare)
    code = ((row << SLOT_BITS | slot_a) << SLOT_BITS | slot_b) + 1
    code = jnp.where(has_a, code, 0).reshape(chunks, -1)
    entries = code.shape[1]
    length = -(-entries // UNROLL) * UNROLL + UNROLL
    at = jnp.arange(entries, dtype=jnp.int32)
    place = jnp.sum(((at[None, :] < at[:, None]) & (code > 0)[:, None, :]).astype(jnp.int32), axis=2)
    place = jnp.where(code > 0, place, -1)
    slots = jnp.arange(length, dtype=jnp.int32)
    packed = jnp.sum(jnp.where(place[:, None, :] == slots[:, None], code[:, None, :], 0), axis=2)
    spare = spare[:, :, 0, 0]
    packed = jnp.where(packed > 0, packed - 1, spare << SLOT_BITS | spare)
    pieces = row_units * unit // piece
    begin = jnp.arange(pieces, dtype=jnp.int32) * (entries // pieces)
    upto = jnp.sum(
        ((at[None, :] < begin[:, None] + entries // pieces) & (code > 0)[:, None, :]).astype(jnp.int32), axis=2
    )
    last = jnp.arange(pieces) == pieces - 1
    ends = jnp.where(last, -(-upto // UNROLL), upto // UNROLL).astype(jnp.int32)
    return ends, packed


def in_vmem(x):
    return pltpu.with_memory_space_constraint(x, pltpu.VMEM)


def score_part(lists, eigen, query_grads, shards, places, near, mapping, base, unit, piece, first_col, width):
    queries = query_grads.shape[0]
    rows = eigen.shape[0]
    token_space = shards[0].shape[1] * len(shards)
    tokens = near.shape[0]
    col_blocks = width // BLOCK
    kernel = functools.partial(score_kernel, unit, piece, first_col, len(shards), base is not None)
    extra = [] if base is None else [base]
    vmem, hbm = pl.BlockSpec(memory_space=pltpu.VMEM), pl.BlockSpec(memory_space=pl.ANY)
    return pl.pallas_call(
        kernel,
        in_specs=[pl.BlockSpec(memory_space=pltpu.SMEM)] * 3 + [hbm, hbm] + [vmem] * (2 + len(extra) + len(shards)),
        out_specs=vmem,
        scratch_shapes=[
            pltpu.VMEM((rows, width), jnp.bfloat16),
            pltpu.VMEM(query_grads.shape, jnp.bfloat16),
            pltpu.VMEM((queries * col_blocks + 1, token_space, BLOCK), jnp.bfloat16),
            pltpu.VMEM((rows // unit, tokens, unit), jnp.bfloat16),
            pltpu.VMEM((queries * col_blocks + 1, tokens, BLOCK), jnp.float32),
            pltpu.SemaphoreType.DMA((2, rows // piece)),
            *[pltpu.VMEM((2, unit, BLOCK), jnp.bfloat16)] * UNROLL,
        ],
        out_shape=jax.ShapeDtypeStruct((queries, mapping.shape[1]), jnp.float32),
        compiler_params=pltpu.CompilerParams(vmem_limit_bytes=48 << 20),
    )(places, *lists, eigen, query_grads, *map(in_vmem, (near, mapping, *extra, *shards)))


def is_small_power(n):
    return n in (1, 2, 4)


def exchange(make, axis, n):
    got = [make(0)]
    for k in range(1, n):
        payload = make(k)
        got.append(lax.ppermute(payload, axis, [(s, s ^ k) for s in range(n)]))
    return got


def relay_exchange(mine, axis):
    far = lax.ppermute(mine, axis, [(0, 2), (2, 0), (1, 3), (3, 1)])
    near = lax.ppermute(mine, axis, [(0, 1), (1, 0), (2, 3), (3, 2)])
    middle = lax.ppermute(mine, axis, [(1, 2), (2, 1)])
    ends = lax.ppermute(far, axis, [(2, 3), (1, 0)])
    return [mine, near, far, middle, ends]


def scores_of(n_out, n_inp, acts_rot, grads_rot, query_grads, query_acts, eigen, block_mask, order, segment_ids):
    rows, cols = eigen.shape
    queries = block_mask.shape[0]
    held = acts_rot.shape[0]
    tokens = order.shape[0]
    at_out, at_inp = lax.axis_index("out"), lax.axis_index("inp")
    unit = math.gcd(rows, BLOCK)
    tile = max(t for t in range(unit, 512 + 1, unit) if rows % t == 0 and (t % BLOCK == 0 or t == rows))
    first = cols // BLOCK * FIRST_SHARE // 16 * BLOCK
    widths = (first, cols - first)
    begins = (0, first)
    chunks = len(widths)
    row_units = rows // unit
    direct = is_small_power(n_out) and is_small_power(n_inp)
    t = jnp.arange(tokens, dtype=jnp.int32)

    if direct:
        near = exchange(
            lambda k: jnp.concatenate(
                [lax.dynamic_slice_in_dim(grads_rot, (at_out ^ k) * rows, rows, 1), acts_rot], axis=1
            ),
            "out", n_out,
        )
        sent = [query_acts[:, :, b : b + w] for b, w in zip(begins, widths)]
        places = [at_out ^ jnp.arange(n_out, dtype=jnp.int32)] * chunks
        if n_out == 4:
            shards = [relay_exchange(sent[0], "out")]
            other = at_out ^ 3
            inner = (at_out == 1) | (at_out == 2)
            places[0] = jnp.stack(
                [at_out, at_out ^ 1, at_out ^ 2, jnp.where(inner, other, 4), jnp.where(inner, 4, other)]
            ).astype(jnp.int32)
        else:
            shards = [exchange(lambda k: sent[0], "out", n_out)]
        shards.append(exchange(lambda k: sent[1], "out", n_out))
    else:
        spread = lax.all_to_all(grads_rot[None], "out", split_axis=2, concat_axis=0, tiled=True)
        grads = lax.all_gather(spread, "inp", axis=1, tiled=True).reshape(-1, rows)
        whole_acts = lax.all_gather(acts_rot, ("out", "inp"), axis=0, tiled=True)
        acts = lax.dynamic_slice_in_dim(whole_acts, at_inp * cols, cols, 1)
        near = jnp.concatenate([grads, acts], axis=1)
        whole = lax.all_gather(query_acts, "out", axis=1, tiled=True)
        shards = [[whole[:, :, begins[c] : begins[c] + widths[c]]] for c in range(chunks)]
        places = [jnp.zeros((1,), jnp.int32)] * chunks

    if direct:
        near = jnp.concatenate(near, axis=0)
        near, block_mask = lax.optimization_barrier((near, block_mask))
    if unit < BLOCK:
        query_grads = query_grads.reshape(queries, -1, row_units, unit).transpose(0, 2, 1, 3)

    row_at = at_out * rows
    if rows % BLOCK == 0:
        band = lax.dynamic_slice_in_dim(block_mask, row_at // BLOCK, row_units, 1)
    else:
        band = jnp.take(block_mask, (row_at + unit * jnp.arange(row_units)) // BLOCK, axis=1)
    band = lax.dynamic_slice_in_dim(band, at_inp * (cols // BLOCK), cols // BLOCK, 2) > 0
    ends, packed = block_lists(band, unit, tile, [w // BLOCK for w in widths])

    if direct:
        both = exchange(
            lambda k: jnp.concatenate(
                [near[:, :rows], lax.dynamic_slice_in_dim(near, rows + (at_inp ^ k) * cols, cols, 1)],
                axis=1,
            ),
            "inp", n_inp,
        )
        near = jnp.concatenate(both, axis=0)
        per_inp = held * n_out
        from_inp = at_inp ^ (t // per_inp)
        from_out = at_out ^ (t % per_inp // held)
        arrived = (from_out * n_inp + from_inp) * held + t % held
    else:
        arrived = t
    position = jnp.sum(jnp.where(arrived[:, None] == t[None, :], order[None, :], 0), axis=1)
    sequence = jnp.sum(jnp.where(position[:, None] == t[None, :], segment_ids[None, :], 0), axis=1)
    reach = -(-(tokens + SEQS) // BLOCK) * BLOCK
    column = jnp.arange(reach, dtype=jnp.int32)[None, :]
    mapping = (
        (column == position[:, None]) | (column == tokens + sequence[:, None])
    ).astype(jnp.float32)

    scores = None
    for c in range(chunks):
        scores = score_part(
            (ends[c], packed[c]), eigen, query_grads, shards[c], places[c], near, mapping, scores,
            unit, tile, begins[c], widths[c],
        )
    if direct:
        for axis, n in (("inp", n_inp), ("out", n_out)):
            k = 1
            while k < n:
                scores = scores + lax.ppermute(scores, axis, [(s, s ^ k) for s in range(n)])
                k *= 2
    else:
        scores = lax.psum(scores, ("out", "inp"))
    return scores[:, :tokens], scores[:, tokens : tokens + SEQS]


def solution(mesh):
    in_specs = (
        P(("groups", "out", "inp"), None),
        P(("groups", "out", "inp"), None),
        P("groups", None, "out"),
        P("groups", "out", "inp"),
        P("out", "inp"),
        P("groups", None, None),
        P("groups"),
        P("groups"),
    )
    out_specs = (P(None, "groups"), P("groups", None))
    return jax.shard_map(
        functools.partial(scores_of, mesh.shape["out"], mesh.shape["inp"]),
        mesh=mesh, in_specs=in_specs, out_specs=out_specs, check_vma=False,
    )
```
